128 devices in a mesh: dish: 16 (over y, z_hi, core), chan: 8 (over z_lo, x).
Axes of the slice: x: 4, y: 4, z: 4 (z_hi: 2, z_lo: 2; z = z_hi * 2 + z_lo), core: 2. Of those that a mesh axis runs over, the one named last changes fastest.
Arguments:
- samples: bfloat16 [1024, 1024, 1024], P('chan', 'dish'), may hold values from -6 to 6
- delays: float32 [512, 1024], replicated, may hold values from -32 to 32
- loading: float32 [128], replicated, may hold values from 0.05 to 0.5
- chan_index: int32 [128], replicated, may hold values from 1 to 511, as said below
- dish_map: int32 [1024], replicated, may hold values from 0 to 1023, as said below
- steer_index: int32 [128], replicated, may hold values from 0 to 511
Outputs:
- beams: float32 [128, 2, 1024, 128], P('dish', None, 'chan')
The draws below stay inside these ranges and needn't reach their ends.
Inputs may be any that keep to these rules, and one draw needn't show every extreme that they name: `chan_index`: 128 distinct channel numbers; 1 and 511 are among them. `dish_map`: each of the 1024 dishes once.
All inputs are finite; a program needn't handle non-finite values.
Results may differ from the reference program's by a relative error of at most 0.017.
Values may be sent and summed in bfloat16 or wider, within the bound.
No kernel may reach another device: no remote copies, remote signals or barrier semaphores. Data moves between devices by JAX's collectives and lax.ppermute only.
A program may use at most 128 MiB of HBM per device.

```python
import math
import jax
import jax.numpy as jnp
from jax import lax

NDISH = 1024
NSAMP = 1024
NCHAN = 512
BEAMS = 128
NDIR = 512
ITERS = 4
FRAMES = 1024
SEL = 128


def draw_common(key):
    middle = jax.random.permutation(jax.random.fold_in(key, 1), NCHAN - 3)[:SEL - 2].astype(jnp.int32) + 2
    ends = jnp.array([1, NCHAN - 1], dtype=jnp.int32)
    values = jnp.concatenate([ends, middle])
    order = jax.random.permutation(jax.random.fold_in(key, 2), SEL)
    channels = values[order].astype(jnp.int32)
    dishes = jax.random.permutation(jax.random.fold_in(key, 3), NDISH).astype(jnp.int32)
    raw_steer = jax.random.randint(jax.random.fold_in(key, 4), (BEAMS,), 0, NDIR).astype(jnp.int32)
    spots = jax.random.permutation(jax.random.fold_in(key, 5), BEAMS)[:2].astype(jnp.int32)
    places = jnp.arange(BEAMS, dtype=jnp.int32)
    steering = jnp.where(places == spots[0], 0, jnp.where(places == spots[1], NDIR - 1, raw_steer)).astype(jnp.int32)
    reach = 1.0 * (NSAMP // 32)
    delay_table = jax.random.uniform(jax.random.fold_in(key, 6), (NDIR, NDISH), jnp.float32, -reach, reach)
    return (channels, dishes, steering, delay_table)


def draw_chan_index(key, part):
    return draw_common(key)[0]


def draw_dish_map(key, part):
    return draw_common(key)[1]


def draw_steer_index(key, part):
    return draw_common(key)[2]


def draw_delays(key, part):
    return draw_common(key)[3]


def draw_samples(key, part):
    channels, dishes, steering, delay_table = draw_common(key)
    noise = jax.random.normal(jax.random.fold_in(key, 20), (FRAMES, NDISH, NSAMP), jnp.float32)
    level_low = 1.0
    level_high = 1.6
    tone_count = max(2, SEL // 16)
    picks = jax.random.randint(jax.random.fold_in(key, 21), (tone_count,), 0, BEAMS)
    levels = jax.random.uniform(jax.random.fold_in(key, 22), (tone_count,), jnp.float32, level_low, level_high)
    gains = jax.random.normal(jax.random.fold_in(key, 23), (tone_count, 2, FRAMES), jnp.float32) * math.sqrt(0.5)
    positions = jnp.arange(NSAMP, dtype=jnp.int32)
    total = noise
    for tone in range(tone_count):
        bin_number = channels[tone]
        direction = steering[picks[tone]]
        lags = jnp.take(jnp.take(delay_table, direction, axis=0), dishes, axis=0)
        base = (positions * bin_number % NSAMP).astype(jnp.float32) * (2.0 * math.pi / NSAMP)
        shift = bin_number.astype(jnp.float32) * lags * (2.0 * math.pi / NSAMP)
        angle = base[None, :] - shift[:, None]
        amplitude = levels[tone] * (2.0 / math.sqrt(NSAMP))
        cosine = jnp.cos(angle)[None, :, :]
        sine = jnp.sin(angle)[None, :, :]
        total = total + amplitude * (gains[tone, 0][:, None, None] * cosine - gains[tone, 1][:, None, None] * sine)
    return jnp.clip(total, -6.0, 6.0).astype(jnp.bfloat16)


def setup_inputs(seed: int = 0) -> dict:
    arg_keys = jax.random.split(jax.random.key(seed), 7)
    samples = draw_samples(jax.random.fold_in(arg_keys[6], 71), 0)
    delays = draw_delays(jax.random.fold_in(arg_keys[6], 71), 0)
    loading = jnp.clip(jnp.exp(jax.random.uniform(arg_keys[2], (SEL,), jnp.float32, math.log(0.05), math.log(0.5))), 0.05, 0.5)
    chan_index = draw_chan_index(jax.random.fold_in(arg_keys[6], 71), 0)
    dish_map = draw_dish_map(jax.random.fold_in(arg_keys[6], 71), 0)
    steer_index = draw_steer_index(jax.random.fold_in(arg_keys[6], 71), 0)
    return {"samples": samples, "delays": delays, "loading": loading, "chan_index": chan_index, "dish_map": dish_map, "steer_index": steer_index}


def build_table(chan_index, sample_count):
    positions = jnp.arange(sample_count, dtype=jnp.int32)
    product = positions[:, None] * chan_index[None, :] % sample_count
    angle = product.astype(jnp.float32) * (2.0 * math.pi / sample_count)
    scaling = 1.0 / math.sqrt(sample_count)
    table = jnp.concatenate([jnp.cos(angle) * scaling, -jnp.sin(angle) * scaling], axis=1)
    return table.astype(jnp.bfloat16)

def solve_channel(real_part, imag_part, bin_number, delta, delay_rows, sample_count):
    dish_total = real_part.shape[1]
    beam_count = delay_rows.shape[1]
    stacked = jnp.concatenate([real_part, imag_part], axis=0)
    rotated = jnp.concatenate([imag_part, -real_part], axis=0)
    contract = (((0,), (0,)), ((), ()))
    cov_real = lax.dot_general(stacked, stacked, contract, preferred_element_type=jnp.float32)
    cov_imag = lax.dot_general(rotated, stacked, contract, preferred_element_type=jnp.float32)
    scale_mean = jnp.trace(cov_real) / dish_total + 1e-06
    frobenius = jnp.sum(cov_real * cov_real) + jnp.sum(cov_imag * cov_imag)
    lower = delta
    upper = delta + jnp.sqrt(dish_total + frobenius / (scale_mean * scale_mean))
    center = 0.5 * (upper + lower)
    half_width = 0.5 * (upper - lower)
    sigma = center / half_width
    packed_real = cov_real.astype(jnp.bfloat16)
    packed_imag = cov_imag.astype(jnp.bfloat16)
    phase = bin_number.astype(jnp.float32) * delay_rows * (-2.0 * math.pi / sample_count)
    steer_real = jnp.cos(phase)
    steer_imag = jnp.sin(phase)

    def apply_operator(direction_real, direction_imag):
        packed = jnp.concatenate([direction_real, direction_imag], axis=1).astype(jnp.bfloat16)
        first = jnp.dot(packed_real, packed, preferred_element_type=jnp.float32)
        second = jnp.dot(packed_imag, packed, preferred_element_type=jnp.float32)
        out_real = (first[:, :beam_count] - second[:, beam_count:]) / scale_mean + delta * direction_real
        out_imag = (second[:, :beam_count] + first[:, beam_count:]) / scale_mean + delta * direction_imag
        return (out_real, out_imag)
    solution_real = jnp.zeros_like(steer_real)
    solution_imag = jnp.zeros_like(steer_imag)
    residual_real = steer_real
    residual_imag = steer_imag
    ratio_now = 1.0 / sigma
    direction_real = steer_real / center
    direction_imag = steer_imag / center
    for step in range(ITERS):
        solution_real = solution_real + direction_real
        solution_imag = solution_imag + direction_imag
        image_real, image_imag = apply_operator(direction_real, direction_imag)
        residual_real = residual_real - image_real
        residual_imag = residual_imag - image_imag
        if step + 1 < ITERS:
            ratio_next = 1.0 / (2.0 * sigma - ratio_now)
            direction_real = ratio_next * ratio_now * direction_real + 2.0 * ratio_next / half_width * residual_real
            direction_imag = ratio_next * ratio_now * direction_imag + 2.0 * ratio_next / half_width * residual_imag
            ratio_now = ratio_next
    power = lax.optimization_barrier(jnp.mean(solution_real * solution_real + solution_imag * solution_imag, axis=0)) + 1e-06
    factor = lax.rsqrt(power * dish_total)
    return ((solution_real * factor).astype(jnp.bfloat16), (solution_imag * factor).astype(jnp.bfloat16))

def form_beams(real_part, imag_part, weight_real, weight_imag):
    joined = jnp.concatenate([real_part, imag_part], axis=1)
    flipped = jnp.concatenate([imag_part, -real_part], axis=1)
    weight_joined = jnp.concatenate([weight_real, weight_imag], axis=0)
    real_beam = jnp.dot(joined, weight_joined, preferred_element_type=jnp.float32)
    imag_beam = jnp.dot(flipped, weight_joined, preferred_element_type=jnp.float32)
    return jnp.stack([real_beam, imag_beam], axis=0)

def reference(samples, delays, loading, chan_index, dish_map, steer_index):
    table = build_table(chan_index, NSAMP)
    flat = samples.reshape(FRAMES * NDISH, NSAMP)
    spectra = jnp.dot(flat, table, preferred_element_type=jnp.float32).astype(jnp.bfloat16)
    spectra = jnp.transpose(spectra.reshape(FRAMES, NDISH, 2, SEL), (3, 2, 0, 1))
    delay_rows = jnp.take(jnp.take(delays, steer_index, axis=0), dish_map, axis=1).T

    def per_channel(items):
        spectrum, bin_number, delta = items
        weight_real, weight_imag = solve_channel(spectrum[0], spectrum[1], bin_number, delta, delay_rows, NSAMP)
        return form_beams(spectrum[0], spectrum[1], weight_real, weight_imag)
    return lax.map(per_channel, (spectra, chan_index, loading))
```

```python
import functools
import math

import jax
import jax.numpy as jnp
from jax import lax
from jax.experimental import pallas as pl
from jax.experimental.pallas import tpu as pltpu
from jax.sharding import PartitionSpec as P

ITERS = 4
LANES = 128
NT = (((1,), (1,)), ((), ()))


def sincos_turns(turns):
    quarter = jnp.round(turns * 4.0)
    angle = (turns - quarter * 0.25) * (2.0 * math.pi)
    square = angle * angle
    sine = angle * (
        1.0
        + square
        * (-1.0 / 6 + square * (1.0 / 120 + square * (-1.0 / 5040 + square * (1.0 / 362880))))
    )
    cosine = 1.0 + square * (
        -0.5
        + square
        * (
            1.0 / 24
            + square * (-1.0 / 720 + square * (1.0 / 40320 + square * (-1.0 / 3628800)))
        )
    )
    phase = quarter.astype(jnp.int32) & 3
    odd = (phase & 1) == 1
    cos_mag = jnp.where(odd, sine, cosine)
    sin_mag = jnp.where(odd, cosine, sine)
    cos_neg = (phase == 1) | (phase == 2)
    sin_neg = phase >= 2
    return jnp.where(cos_neg, -cos_mag, cos_mag), jnp.where(sin_neg, -sin_mag, sin_mag)


def spectra_kernel(chan_ref, samples_ref, out_ref, table_ref, stage_ref):
    selected = chan_ref.shape[1]
    sample_count = samples_ref.shape[3]
    pairs = samples_ref.shape[1]

    @pl.when(pl.program_id(0) == 0)
    def _():
        chan = jnp.broadcast_to(chan_ref[...].astype(jnp.float32), (selected, selected)).T
        position = lax.broadcasted_iota(jnp.int32, (selected, LANES), 1).astype(jnp.float32)
        turns = chan * position * (1.0 / sample_count)
        cosine, sine = sincos_turns(turns - jnp.round(turns))
        scaling = 1.0 / math.sqrt(sample_count)
        cosine = cosine * scaling
        sine = sine * scaling
        jump = chan * (float(LANES) / sample_count)
        jump_cos, jump_sin = sincos_turns(jump - jnp.round(jump))
        for block in range(sample_count // LANES):
            span = slice(block * LANES, (block + 1) * LANES)
            table_ref[0:selected, span] = cosine.astype(jnp.bfloat16)
            table_ref[selected : 2 * selected, span] = (-sine).astype(jnp.bfloat16)
            cosine, sine = (
                cosine * jump_cos - sine * jump_sin,
                sine * jump_cos + cosine * jump_sin,
            )

    table = table_ref[...]
    for pair in range(0, pairs, 2):
        rows = jnp.concatenate(
            [
                samples_ref[0, pair],
                samples_ref[1, pair],
                samples_ref[0, pair + 1],
                samples_ref[1, pair + 1],
            ],
            axis=0,
        )
        values = lax.dot_general(table, rows, NT, preferred_element_type=jnp.float32)
        for extra in range(2):
            for part in range(2):
                stage_ref[pl.ds(part * pairs + pair + extra, selected, stride=2 * pairs), :] = (
                    values[
                        part * selected : (part + 1) * selected,
                        extra * LANES : (extra + 1) * LANES,
                    ]
                )
    out_ref[...] = stage_ref[...].reshape(selected, 2, pairs, LANES).astype(jnp.bfloat16)


def spectra_call(samples, chan_index):
    frames, dishes, sample_count = samples.shape
    selected = chan_index.shape[0]
    half = frames // 2
    pairs = 16
    return pl.pallas_call(
        spectra_kernel,
        out_shape=jax.ShapeDtypeStruct((selected, 2, half, LANES), jnp.bfloat16),
        grid=(half // pairs,),
        in_specs=[
            pl.BlockSpec((1, selected), lambda i: (0, 0)),
            pl.BlockSpec((2, pairs, dishes, sample_count), lambda i: (0, i, 0, 0)),
        ],
        out_specs=pl.BlockSpec((selected, 2, pairs, LANES), lambda i: (0, 0, i, 0)),
        scratch_shapes=[
            pltpu.VMEM((2 * selected, sample_count), jnp.bfloat16),
            pltpu.VMEM((selected * 2 * pairs, LANES), jnp.float32),
        ],
        name="spectra",
    )(chan_index.reshape(1, selected), samples.reshape(2, half, dishes, sample_count))


def solve_kernel(
    sample_count,
    own_ref,
    chan_ref,
    load_ref,
    recv_ref,
    delay_ref,
    out_ref,
    joined_ref,
    turned_ref,
    real_ref,
    imag_ref,
    state_ref,
):
    blocks, groups, _, half, _ = recv_ref.shape
    dish_total, beam_count = delay_ref.shape
    dish_local = dish_total // blocks
    span = groups * half
    frames = 2 * span
    own = own_ref[0]
    delta = load_ref[own]
    bin_number = chan_ref[own].astype(jnp.float32)

    for block in range(blocks):
        rows = slice(block * dish_local, (block + 1) * dish_local)
        for part in range(2):
            piece = recv_ref[block, :, part].reshape(span, LANES)
            flipped = piece.T
            for side in range(2):
                values = flipped[side * dish_local : (side + 1) * dish_local, :]
                first = part * frames + side * span
                joined_ref[rows, first : first + span] = values
                other = (1 - part) * frames + side * span
                turned_ref[rows, other : other + span] = values if part == 1 else -values

    step = 256
    trace = jnp.float32(0.0)
    energy = jnp.float32(0.0)
    for first in range(0, dish_total, step):
        cols = slice(first, first + step)
        right = joined_ref[cols, :]
        cov_real = lax.dot_general(joined_ref[...], right, NT, preferred_element_type=jnp.float32)
        cov_imag = lax.dot_general(turned_ref[...], right, NT, preferred_element_type=jnp.float32)
        diagonal = cov_real[first : first + step, :]
        same = lax.broadcasted_iota(jnp.int32, (step, step), 0) == lax.broadcasted_iota(
            jnp.int32, (step, step), 1
        )
        trace = trace + jnp.sum(jnp.where(same, diagonal, 0.0))
        energy = energy + jnp.sum(cov_real * cov_real + cov_imag * cov_imag)
        real_ref[:, cols] = cov_real.astype(jnp.bfloat16)
        imag_ref[:, cols] = cov_imag.astype(jnp.bfloat16)

    def full(value):
        return jnp.full((1, beam_count), value, jnp.float32)

    scale_mean = full(trace) / dish_total + 1e-06
    load = full(delta)
    upper = load + jnp.sqrt(dish_total + full(energy) / (scale_mean * scale_mean))
    center = 0.5 * (upper + load)
    half_width = 0.5 * (upper - load)
    sigma = center / half_width
    inverse_scale = 1.0 / scale_mean
    inverse_center = 1.0 / center

    turns = bin_number * delay_ref[...] * (-1.0 / sample_count)
    steer_real, steer_imag = sincos_turns(turns - jnp.round(turns))
    sol_real = steer_real * inverse_center
    sol_imag = steer_imag * inverse_center
    res_real, res_imag = steer_real, steer_imag
    dir_real, dir_imag = sol_real, sol_imag
    ratio_now = 1.0 / sigma
    for turn in range(ITERS - 1):
        state_ref[:, 0:beam_count] = dir_real.astype(jnp.bfloat16)
        state_ref[:, beam_count : 2 * beam_count] = dir_imag.astype(jnp.bfloat16)
        packed = state_ref[...]
        first = jnp.dot(real_ref[...], packed, preferred_element_type=jnp.float32)
        second = jnp.dot(imag_ref[...], packed, preferred_element_type=jnp.float32)
        res_real = res_real - (
            (first[:, :beam_count] - second[:, beam_count:]) * inverse_scale + load * dir_real
        )
        res_imag = res_imag - (
            (second[:, :beam_count] + first[:, beam_count:]) * inverse_scale + load * dir_imag
        )
        ratio_next = 1.0 / (2.0 * sigma - ratio_now)
        keep = ratio_next * ratio_now
        gain = 2.0 * ratio_next / half_width
        dir_real = keep * dir_real + gain * res_real
        dir_imag = keep * dir_imag + gain * res_imag
        ratio_now = ratio_next
        sol_real = sol_real + dir_real
        sol_imag = sol_imag + dir_imag

    power = jnp.sum(sol_real * sol_real + sol_imag * sol_imag, axis=0, keepdims=True) / dish_total
    factor = lax.rsqrt((power + 1e-06) * dish_total)
    weight_real = (sol_real * factor).astype(jnp.bfloat16)
    weight_imag = (sol_imag * factor).astype(jnp.bfloat16)

    total = jnp.zeros((span, 4 * beam_count), jnp.float32)
    empty = jnp.zeros((dish_local, 2 * beam_count), jnp.bfloat16)
    for block in range(blocks):
        rows = slice(block * dish_local, (block + 1) * dish_local)
        wr, wi = weight_real[rows, :], weight_imag[rows, :]
        on_real = jnp.concatenate([wr, -wi], axis=1)
        on_imag = jnp.concatenate([wi, wr], axis=1)
        right = jnp.concatenate(
            [
                jnp.concatenate([on_real, empty], axis=1),
                jnp.concatenate([empty, on_real], axis=1),
                jnp.concatenate([on_imag, empty], axis=1),
                jnp.concatenate([empty, on_imag], axis=1),
            ],
            axis=0,
        )
        left = jnp.concatenate(
            [
                recv_ref[block, :, 0].reshape(span, LANES),
                recv_ref[block, :, 1].reshape(span, LANES),
            ],
            axis=1,
        )
        total = total + jnp.dot(left, right, preferred_element_type=jnp.float32)
    for group in range(groups):
        for side in range(2):
            for part in range(2):
                first = (2 * side + part) * beam_count
                out_ref[group, part, side * half : (side + 1) * half, :] = total[
                    group * half : (group + 1) * half, first : first + beam_count
                ].astype(jnp.bfloat16)


def solve_call(sample_count, own, chan_index, loading, received, delay_rows):
    blocks, groups, _, half, _ = received.shape
    dish_total, beam_count = delay_rows.shape
    frames = 2 * groups * half
    smem = pl.BlockSpec(memory_space=pltpu.SMEM)
    vmem = pl.BlockSpec(memory_space=pltpu.VMEM)
    return pl.pallas_call(
        functools.partial(solve_kernel, sample_count),
        out_shape=jax.ShapeDtypeStruct((groups, 2, 2 * half, beam_count), jnp.bfloat16),
        in_specs=[smem, smem, smem, vmem, vmem],
        out_specs=vmem,
        scratch_shapes=[
            pltpu.VMEM((dish_total, 2 * frames), jnp.bfloat16),
            pltpu.VMEM((dish_total, 2 * frames), jnp.bfloat16),
            pltpu.VMEM((dish_total, dish_total), jnp.bfloat16),
            pltpu.VMEM((dish_total, dish_total), jnp.bfloat16),
            pltpu.VMEM((dish_total, 2 * beam_count), jnp.bfloat16),
        ],
        name="solve",
    )(own, chan_index, loading, received, delay_rows)


def local(samples, delays, loading, chan_index, dish_map, steer_index):
    dish_count = lax.axis_size("dish")
    chan_count = lax.axis_size("chan")
    own = (lax.axis_index("dish") * chan_count + lax.axis_index("chan")).reshape(1)
    spectra = spectra_call(samples, chan_index)
    received = lax.all_to_all(spectra, ("dish", "chan"), 0, 0, tiled=True)
    received = received.reshape((dish_count, chan_count) + received.shape[1:])
    delay_rows = jnp.take(jnp.take(delays, steer_index, axis=0), dish_map, axis=1).T
    beams = solve_call(samples.shape[2], own, chan_index, loading, received, delay_rows)
    return lax.all_to_all(beams, "chan", 0, 0, tiled=True).astype(jnp.float32)


def solution(mesh):
    return jax.shard_map(
        local,
        mesh=mesh,
        in_specs=(P("chan", "dish", None), P(), P(), P(), P(), P()),
        out_specs=P("dish", None, "chan", None),
        check_vma=False,
    )
```

```python
import functools
import math

import jax
import jax.numpy as jnp
from jax import lax
from jax.experimental import pallas as pl
from jax.experimental.pallas import tpu as pltpu
from jax.sharding import PartitionSpec as P

ITERS = 4
PIECES = (16, 16, 16, 16)
WIDE = 2
LANES = 128
TILE = 256
NT = (((1,), (1,)), ((), ()))


def sincos_turns(turns):
    quarter = jnp.round(turns * 4.0)
    angle = (turns - quarter * 0.25) * (2.0 * math.pi)
    square = angle * angle
    sine = angle * (
        1.0
        + square
        * (-1.0 / 6 + square * (1.0 / 120 + square * (-1.0 / 5040 + square * (1.0 / 362880))))
    )
    cosine = 1.0 + square * (
        -0.5
        + square
        * (
            1.0 / 24
            + square * (-1.0 / 720 + square * (1.0 / 40320 + square * (-1.0 / 3628800)))
        )
    )
    phase = quarter.astype(jnp.int32) & 3
    odd = (phase & 1) == 1
    cos_mag = jnp.where(odd, sine, cosine)
    sin_mag = jnp.where(odd, cosine, sine)
    cos_neg = (phase == 1) | (phase == 2)
    sin_neg = phase >= 2
    return jnp.where(cos_neg, -cos_mag, cos_mag), jnp.where(sin_neg, -sin_mag, sin_mag)


def spectra_kernel(
    chan_ref, samples_ref, out_ref, table_ref, held_ref, stage_ref, ready_ref, in_sems, out_sems
):
    selected = chan_ref.shape[1]
    sample_count = samples_ref.shape[3]
    half = samples_ref.shape[1]
    groups = out_sems.shape[0]
    pairs = half // groups

    loads = {}
    first = 0
    for piece, size in enumerate(PIECES):
        rows = slice(first, first + size)
        loads[first] = pltpu.make_async_copy(
            samples_ref.at[:, rows], held_ref.at[:, rows], in_sems.at[piece]
        )
        loads[first].start()
        first += size

    chan = jnp.broadcast_to(chan_ref[...].astype(jnp.float32), (selected, selected)).T
    position = lax.broadcasted_iota(jnp.int32, (selected, LANES), 1).astype(jnp.float32)
    turns = chan * position * (1.0 / sample_count)
    cosine, sine = sincos_turns(turns - jnp.round(turns))
    scaling = 1.0 / math.sqrt(sample_count)
    cosine = cosine * scaling
    sine = sine * scaling
    jump = chan * (float(LANES) / sample_count)
    jump_cos, jump_sin = sincos_turns(jump - jnp.round(jump))
    for block in range(sample_count // LANES):
        span = slice(block * LANES, (block + 1) * LANES)
        table_ref[0:selected, span] = cosine.astype(jnp.bfloat16)
        table_ref[selected : 2 * selected, span] = (-sine).astype(jnp.bfloat16)
        cosine, sine = (
            cosine * jump_cos - sine * jump_sin,
            sine * jump_cos + cosine * jump_sin,
        )

    stores = []
    stride = stage_ref.shape[1] // selected
    for group in range(groups):
        slot = group % 2
        for pair in range(0, pairs, WIDE):
            place = group * pairs + pair
            if place in loads:
                loads[place].wait()
            rows = jnp.concatenate(
                [held_ref[side, place + extra] for extra in range(WIDE) for side in range(2)],
                axis=0,
            )
            values = lax.dot_general(
                table_ref[...], rows, NT, preferred_element_type=jnp.float32
            )
            for extra in range(WIDE):
                for part in range(2):
                    stage_ref[
                        slot, pl.ds(part * pairs + pair + extra, selected, stride=stride), :
                    ] = values[
                        part * selected : (part + 1) * selected,
                        extra * LANES : (extra + 1) * LANES,
                    ]
        rows = slice(group * pairs, (group + 1) * pairs)
        staged = stage_ref[slot].reshape(selected, stride, LANES)[:, : 2 * pairs]
        ready_ref[:, :, rows] = staged.astype(jnp.bfloat16).reshape(selected, 2, pairs, LANES)
        stores.append(
            pltpu.make_async_copy(
                ready_ref.at[:, :, rows], out_ref.at[:, :, rows], out_sems.at[group]
            )
        )
        stores[-1].start()
    for store in stores:
        store.wait()


def spectra_call(samples, chan_index):
    frames, dishes, sample_count = samples.shape
    selected = chan_index.shape[0]
    half = frames // 2
    groups = 4
    stride = 2 * half // groups + 8
    hbm = pl.BlockSpec(memory_space=pl.ANY)
    return pl.pallas_call(
        spectra_kernel,
        out_shape=jax.ShapeDtypeStruct((selected, 2, half, LANES), jnp.bfloat16),
        in_specs=[pl.BlockSpec(memory_space=pltpu.VMEM), hbm],
        out_specs=hbm,
        scratch_shapes=[
            pltpu.VMEM((2 * selected, sample_count), jnp.bfloat16),
            pltpu.VMEM((2, half, dishes, sample_count), jnp.bfloat16),
            pltpu.VMEM((2, selected * stride, LANES), jnp.float32),
            pltpu.VMEM((selected, 2, half, LANES), jnp.bfloat16),
            pltpu.SemaphoreType.DMA((len(PIECES),)),
            pltpu.SemaphoreType.DMA((groups,)),
        ],
        name="spectra",
    )(chan_index.reshape(1, selected), samples.reshape(2, half, dishes, sample_count))


def solve_kernel(
    sample_count,
    own_ref,
    chan_ref,
    load_ref,
    recv_ref,
    delay_ref,
    out_ref,
    held_ref,
    joined_ref,
    turned_ref,
    real_ref,
    imag_ref,
    packed_ref,
    sol_ref,
    res_ref,
    dir_ref,
    weight_ref,
    sems,
):
    blocks, groups, _, half, _ = recv_ref.shape
    dish_total, beam_count = delay_ref.shape
    dish_local = dish_total // blocks
    span = groups * half
    frames = 2 * span
    own = own_ref[0]
    delta = load_ref[own]
    bin_number = chan_ref[own].astype(jnp.float32)
    on_real, on_imag = slice(0, beam_count), slice(beam_count, 2 * beam_count)

    loads = []
    each = blocks // sems.shape[0]
    for index in range(sems.shape[0]):
        part = slice(index * each, (index + 1) * each)
        loads.append(pltpu.make_async_copy(recv_ref.at[part], held_ref.at[part], sems.at[index]))
        loads[-1].start()

    turns = bin_number * delay_ref[...] * (-1.0 / sample_count)
    steer_real, steer_imag = sincos_turns(turns - jnp.round(turns))
    res_ref[:, on_real] = steer_real
    res_ref[:, on_imag] = steer_imag

    for block in range(blocks):
        if block % each == 0:
            loads[block // each].wait()
        rows = slice(block * dish_local, (block + 1) * dish_local)
        for part in range(2):
            flipped = held_ref[block, :, part].reshape(span, LANES).T
            for side in range(2):
                values = flipped[side * dish_local : (side + 1) * dish_local, :]
                first = part * frames + side * span
                joined_ref[rows, first : first + span] = values
                other = (1 - part) * frames + side * span
                turned_ref[rows, other : other + span] = values if part == 1 else -values

    tiles = [slice(first, first + TILE) for first in range(0, dish_total, TILE)]
    same = lax.broadcasted_iota(jnp.int32, (TILE, TILE), 0) == lax.broadcasted_iota(
        jnp.int32, (TILE, TILE), 1
    )
    trace = jnp.zeros((1, TILE), jnp.float32)
    energy = jnp.zeros((1, TILE), jnp.float32)
    for index, cols in enumerate(tiles):
        right = joined_ref[cols, :]
        top = cols.stop
        cov_real = lax.dot_general(
            joined_ref[0:top, :], right, NT, preferred_element_type=jnp.float32
        )
        cov_imag = lax.dot_general(
            turned_ref[0:top, :], right, NT, preferred_element_type=jnp.float32
        )
        square = cov_real * cov_real + cov_imag * cov_imag
        trace = trace + jnp.sum(jnp.where(same, cov_real[cols, :], 0.0), axis=0, keepdims=True)
        energy = energy + jnp.sum(square[cols, :], axis=0, keepdims=True)
        packed_real = cov_real.astype(jnp.bfloat16)
        packed_imag = cov_imag.astype(jnp.bfloat16)
        real_ref[0:top, cols] = packed_real
        imag_ref[0:top, cols] = packed_imag
        if index:
            energy = energy + 2.0 * jnp.sum(square[0 : cols.start, :], axis=0, keepdims=True)
        for rows in tiles[:index]:
            real_ref[cols, rows] = packed_real[rows, :].T
            imag_ref[cols, rows] = -packed_imag[rows, :].T

    def full(value):
        return jnp.full((1, 2 * beam_count), value, jnp.float32)

    scale_mean = full(jnp.sum(trace)) / dish_total + 1e-06
    load = full(delta)
    upper = load + jnp.sqrt(dish_total + full(jnp.sum(energy)) / (scale_mean * scale_mean))
    center = 0.5 * (upper + load)
    half_width = 0.5 * (upper - load)
    sigma = center / half_width
    inverse_scale = (1.0 / scale_mean)[:, on_real]
    inverse_center = 1.0 / center

    ratio_now = 1.0 / sigma
    power = jnp.zeros((1, 2 * beam_count), jnp.float32)
    for rows in tiles:
        first = res_ref[rows, :] * inverse_center
        sol_ref[rows, :] = first
        dir_ref[rows, :] = first
        packed_ref[0, rows, :] = first.astype(jnp.bfloat16)
    for turn in range(ITERS - 1):
        ratio_next = 1.0 / (2.0 * sigma - ratio_now)
        keep = ratio_next * ratio_now
        gain = 2.0 * ratio_next / half_width
        ratio_now = ratio_next
        packed = packed_ref[turn % 2]
        for rows in tiles:
            by_real = jnp.dot(real_ref[rows, :], packed, preferred_element_type=jnp.float32)
            by_imag = jnp.dot(imag_ref[rows, :], packed, preferred_element_type=jnp.float32)
            image = jnp.concatenate(
                [
                    (by_real[:, on_real] - by_imag[:, on_imag]) * inverse_scale,
                    (by_imag[:, on_real] + by_real[:, on_imag]) * inverse_scale,
                ],
                axis=1,
            )
            old = dir_ref[rows, :]
            residual = res_ref[rows, :] - (image + load * old)
            new = keep * old + gain * residual
            total = sol_ref[rows, :] + new
            sol_ref[rows, :] = total
            if turn + 2 < ITERS:
                res_ref[rows, :] = residual
                dir_ref[rows, :] = new
                packed_ref[(turn + 1) % 2, rows, :] = new.astype(jnp.bfloat16)
            else:
                power = power + jnp.sum(total * total, axis=0, keepdims=True)

    power = (power[:, on_real] + power[:, on_imag]) / dish_total
    factor = lax.rsqrt((power + 1e-06) * dish_total)
    for rows in tiles:
        weight_real = (sol_ref[rows, on_real] * factor).astype(jnp.bfloat16).T
        weight_imag = (sol_ref[rows, on_imag] * factor).astype(jnp.bfloat16).T
        weight_ref[0, on_real, rows] = weight_real
        weight_ref[0, on_imag, rows] = -weight_imag
        weight_ref[1, on_real, rows] = weight_imag
        weight_ref[1, on_imag, rows] = weight_real

    for side in range(2):
        for first in range(0, span, TILE):
            place = side * span + first
            beams = jnp.dot(
                weight_ref[0],
                joined_ref[:, place : place + TILE],
                preferred_element_type=jnp.float32,
            ) + jnp.dot(
                weight_ref[1],
                joined_ref[:, frames + place : frames + place + TILE],
                preferred_element_type=jnp.float32,
            )
            beams = beams.astype(jnp.bfloat16)
            for part, lanes in enumerate((on_real, on_imag)):
                flipped = beams[lanes, :].T
                for group in range(TILE // half):
                    out_ref[first // half + group, part, side * half : (side + 1) * half, :] = (
                        flipped[group * half : (group + 1) * half, :]
                    )


def solve_call(sample_count, own, chan_index, loading, received, delay_rows):
    blocks, groups, _, half, _ = received.shape
    dish_total, beam_count = delay_rows.shape
    frames = 2 * groups * half
    smem = pl.BlockSpec(memory_space=pltpu.SMEM)
    vmem = pl.BlockSpec(memory_space=pltpu.VMEM)
    hbm = pl.BlockSpec(memory_space=pl.ANY)
    wide = (dish_total, 2 * beam_count)
    return pl.pallas_call(
        functools.partial(solve_kernel, sample_count),
        out_shape=jax.ShapeDtypeStruct((groups, 2, 2 * half, beam_count), jnp.bfloat16),
        in_specs=[smem, smem, smem, hbm, vmem],
        out_specs=vmem,
        scratch_shapes=[
            pltpu.VMEM(received.shape, jnp.bfloat16),
            pltpu.VMEM((dish_total, 2 * frames), jnp.bfloat16),
            pltpu.VMEM((dish_total, 2 * frames), jnp.bfloat16),
            pltpu.VMEM((dish_total, dish_total), jnp.bfloat16),
            pltpu.VMEM((dish_total, dish_total), jnp.bfloat16),
            pltpu.VMEM((2,) + wide, jnp.bfloat16),
            pltpu.VMEM(wide, jnp.float32),
            pltpu.VMEM(wide, jnp.float32),
            pltpu.VMEM(wide, jnp.float32),
            pltpu.VMEM((2, 2 * beam_count, dish_total), jnp.bfloat16),
            pltpu.SemaphoreType.DMA((4,)),
        ],
        name="solve",
    )(own, chan_index, loading, received, delay_rows)


def local(samples, delays, loading, chan_index, dish_map, steer_index):
    dish_count = lax.axis_size("dish")
    chan_count = lax.axis_size("chan")
    own = (lax.axis_index("dish") * chan_count + lax.axis_index("chan")).reshape(1)
    spectra = spectra_call(samples, chan_index)
    received = lax.all_to_all(spectra, ("dish", "chan"), 0, 0, tiled=True)
    received = received.reshape((dish_count, chan_count) + received.shape[1:])
    delay_rows = jnp.take(jnp.take(delays, steer_index, axis=0), dish_map, axis=1).T
    beams = solve_call(samples.shape[2], own, chan_index, loading, received, delay_rows)
    return lax.all_to_all(beams, "chan", 0, 0, tiled=True).astype(jnp.float32)


def solution(mesh):
    return jax.shard_map(
        local,
        mesh=mesh,
        in_specs=(P("chan", "dish", None), P(), P(), P(), P(), P()),
        out_specs=P("dish", None, "chan", None),
        check_vma=False,
    )
```

```python
import functools
import math

import jax
import jax.numpy as jnp
from jax import lax
from jax.experimental import pallas as pl
from jax.experimental.pallas import tpu as pltpu
from jax.sharding import PartitionSpec as P

ITERS = 4
PIECES = (16, 16, 16, 16)
WIDE = 2
LANES = 128
TILE = 256
NT = (((1,), (1,)), ((), ()))


def sincos_turns(turns):
    quarter = jnp.round(turns * 4.0)
    angle = (turns - quarter * 0.25) * (2.0 * math.pi)
    square = angle * angle
    sine = angle * (
        1.0
        + square
        * (-1.0 / 6 + square * (1.0 / 120 + square * (-1.0 / 5040 + square * (1.0 / 362880))))
    )
    cosine = 1.0 + square * (
        -0.5
        + square
        * (
            1.0 / 24
            + square * (-1.0 / 720 + square * (1.0 / 40320 + square * (-1.0 / 3628800)))
        )
    )
    phase = quarter.astype(jnp.int32) & 3
    odd = (phase & 1) == 1
    cos_mag = jnp.where(odd, sine, cosine)
    sin_mag = jnp.where(odd, cosine, sine)
    cos_neg = (phase == 1) | (phase == 2)
    sin_neg = phase >= 2
    return jnp.where(cos_neg, -cos_mag, cos_mag), jnp.where(sin_neg, -sin_mag, sin_mag)


def spectra_kernel(
    chan_ref, samples_ref, out_ref, table_ref, held_ref, stage_ref, ready_ref, in_sems, out_sems
):
    selected = chan_ref.shape[1]
    sample_count = samples_ref.shape[3]
    half = samples_ref.shape[1]
    groups = out_sems.shape[0]
    pairs = half // groups

    loads = {}
    first = 0
    for piece, size in enumerate(PIECES):
        rows = slice(first, first + size)
        loads[first] = pltpu.make_async_copy(
            samples_ref.at[:, rows], held_ref.at[:, rows], in_sems.at[piece]
        )
        loads[first].start()
        first += size

    chan = jnp.broadcast_to(chan_ref[...].astype(jnp.float32), (selected, selected)).T
    position = lax.broadcasted_iota(jnp.int32, (selected, LANES), 1).astype(jnp.float32)
    turns = chan * position * (1.0 / sample_count)
    cosine, sine = sincos_turns(turns - jnp.round(turns))
    scaling = 1.0 / math.sqrt(sample_count)
    cosine = cosine * scaling
    sine = sine * scaling
    jump = chan * (float(LANES) / sample_count)
    jump_cos, jump_sin = sincos_turns(jump - jnp.round(jump))
    for block in range(sample_count // LANES):
        span = slice(block * LANES, (block + 1) * LANES)
        table_ref[0:selected, span] = cosine.astype(jnp.bfloat16)
        table_ref[selected : 2 * selected, span] = (-sine).astype(jnp.bfloat16)
        cosine, sine = (
            cosine * jump_cos - sine * jump_sin,
            sine * jump_cos + cosine * jump_sin,
        )

    stores = []
    stride = stage_ref.shape[1] // selected
    for group in range(groups):
        slot = group % 2
        for pair in range(0, pairs, WIDE):
            place = group * pairs + pair
            if place in loads:
                loads[place].wait()
            rows = jnp.concatenate(
                [held_ref[side, place + extra] for extra in range(WIDE) for side in range(2)],
                axis=0,
            )
            values = lax.dot_general(
                table_ref[...], rows, NT, preferred_element_type=jnp.float32
            )
            for extra in range(WIDE):
                for part in range(2):
                    stage_ref[
                        slot, pl.ds(part * pairs + pair + extra, selected, stride=stride), :
                    ] = values[
                        part * selected : (part + 1) * selected,
                        extra * LANES : (extra + 1) * LANES,
                    ]
        rows = slice(group * pairs, (group + 1) * pairs)
        staged = stage_ref[slot].reshape(selected, stride, LANES)[:, : 2 * pairs]
        ready_ref[:, :, rows] = staged.astype(jnp.bfloat16).reshape(selected, 2, pairs, LANES)
        stores.append(
            pltpu.make_async_copy(
                ready_ref.at[:, :, rows], out_ref.at[:, :, rows], out_sems.at[group]
            )
        )
        stores[-1].start()
    for store in stores:
        store.wait()


def spectra_call(samples, chan_index):
    frames, dishes, sample_count = samples.shape
    selected = chan_index.shape[0]
    half = frames // 2
    groups = 4
    stride = 2 * half // groups + 8
    hbm = pl.BlockSpec(memory_space=pl.ANY)
    return pl.pallas_call(
        spectra_kernel,
        out_shape=jax.ShapeDtypeStruct((selected, 2, half, LANES), jnp.bfloat16),
        in_specs=[pl.BlockSpec(memory_space=pltpu.VMEM), hbm],
        out_specs=hbm,
        scratch_shapes=[
            pltpu.VMEM((2 * selected, sample_count), jnp.bfloat16),
            pltpu.VMEM((2, half, dishes, sample_count), jnp.bfloat16),
            pltpu.VMEM((2, selected * stride, LANES), jnp.float32),
            pltpu.VMEM((selected, 2, half, LANES), jnp.bfloat16),
            pltpu.SemaphoreType.DMA((len(PIECES),)),
            pltpu.SemaphoreType.DMA((groups,)),
        ],
        name="spectra",
    )(chan_index.reshape(1, selected), samples.reshape(2, half, dishes, sample_count))


def solve_kernel(
    sample_count,
    own_ref,
    chan_ref,
    load_ref,
    recv_ref,
    delay_ref,
    out_ref,
    held_ref,
    joined_ref,
    sum_ref,
    diff_ref,
    cross_ref,
    real_ref,
    imag_ref,
    packed_ref,
    sol_ref,
    res_ref,
    dir_ref,
    weight_ref,
    sems,
):
    blocks, groups, _, half, _ = recv_ref.shape
    dish_total, beam_count = delay_ref.shape
    dish_local = dish_total // blocks
    span = groups * half
    frames = 2 * span
    own = own_ref[0]
    delta = load_ref[own]
    bin_number = chan_ref[own].astype(jnp.float32)
    on_real, on_imag = slice(0, beam_count), slice(beam_count, 2 * beam_count)

    loads = []
    each = blocks // sems.shape[0]
    for index in range(sems.shape[0]):
        part = slice(index * each, (index + 1) * each)
        loads.append(pltpu.make_async_copy(recv_ref.at[part], held_ref.at[part], sems.at[index]))
        loads[-1].start()

    turns = bin_number * delay_ref[...] * (-1.0 / sample_count)
    steer_real, steer_imag = sincos_turns(turns - jnp.round(turns))
    res_ref[:, on_real] = steer_real
    res_ref[:, on_imag] = steer_imag

    for block in range(blocks):
        if block % each == 0:
            loads[block // each].wait()
        rows = slice(block * dish_local, (block + 1) * dish_local)
        real_part, imag_part = (
            held_ref[block, :, part].reshape(span, LANES).T for part in range(2)
        )
        for side in range(2):
            inner = slice(side * dish_local, (side + 1) * dish_local)
            cols = slice(side * span, (side + 1) * span)
            joined_ref[rows, side * span : (side + 1) * span] = real_part[inner, :]
            joined_ref[rows, frames + side * span : frames + (side + 1) * span] = imag_part[
                inner, :
            ]
            sum_ref[rows, cols] = real_part[inner, :] + imag_part[inner, :]
            diff_ref[rows, cols] = real_part[inner, :] - imag_part[inner, :]

    tiles = [slice(first, first + TILE) for first in range(0, dish_total, TILE)]
    same = lax.broadcasted_iota(jnp.int32, (TILE, TILE), 0) == lax.broadcasted_iota(
        jnp.int32, (TILE, TILE), 1
    )
    trace = jnp.zeros((1, TILE), jnp.float32)
    energy = jnp.zeros((1, TILE), jnp.float32)
    for index, cols in enumerate(tiles):
        top = cols.stop
        cross_ref[:, cols] = lax.dot_general(
            sum_ref[...], diff_ref[cols, :], NT, preferred_element_type=jnp.float32
        )
        square_imag = lax.dot_general(
            joined_ref[0:top, frames:],
            joined_ref[cols, frames:],
            NT,
            preferred_element_type=jnp.float32,
        )
        for rows in tiles[: index + 1]:
            upper_part = cross_ref[rows, cols]
            lower_part = cross_ref[cols, rows].T
            cov_real = 0.5 * (upper_part + lower_part) + 2.0 * square_imag[rows, :]
            cov_imag = 0.5 * (upper_part - lower_part)
            square = cov_real * cov_real + cov_imag * cov_imag
            share = jnp.sum(square, axis=0, keepdims=True)
            packed_real = cov_real.astype(jnp.bfloat16)
            packed_imag = cov_imag.astype(jnp.bfloat16)
            real_ref[rows, cols] = packed_real
            imag_ref[rows, cols] = packed_imag
            if rows == cols:
                diagonal = jnp.where(same, cov_real, 0.0)
                trace = trace + jnp.sum(diagonal, axis=0, keepdims=True)
                energy = energy + share
            else:
                energy = energy + 2.0 * share
                real_ref[cols, rows] = packed_real.T
                imag_ref[cols, rows] = -packed_imag.T

    def full(value):
        return jnp.full((1, 2 * beam_count), value, jnp.float32)

    scale_mean = full(jnp.sum(trace)) / dish_total + 1e-06
    load = full(delta)
    upper = load + jnp.sqrt(dish_total + full(jnp.sum(energy)) / (scale_mean * scale_mean))
    center = 0.5 * (upper + load)
    half_width = 0.5 * (upper - load)
    sigma = center / half_width
    inverse_scale = (1.0 / scale_mean)[:, on_real]
    inverse_center = 1.0 / center

    ratio_now = 1.0 / sigma
    power = jnp.zeros((1, 2 * beam_count), jnp.float32)
    for rows in tiles:
        first = res_ref[rows, :] * inverse_center
        sol_ref[rows, :] = first
        dir_ref[rows, :] = first
        packed_ref[0, rows, :] = first.astype(jnp.bfloat16)
    for turn in range(ITERS - 1):
        ratio_next = 1.0 / (2.0 * sigma - ratio_now)
        keep = ratio_next * ratio_now
        gain = 2.0 * ratio_next / half_width
        ratio_now = ratio_next
        packed = packed_ref[turn % 2]
        for rows in tiles:
            by_real = jnp.dot(real_ref[rows, :], packed, preferred_element_type=jnp.float32)
            by_imag = jnp.dot(imag_ref[rows, :], packed, preferred_element_type=jnp.float32)
            image = jnp.concatenate(
                [
                    (by_real[:, on_real] - by_imag[:, on_imag]) * inverse_scale,
                    (by_imag[:, on_real] + by_real[:, on_imag]) * inverse_scale,
                ],
                axis=1,
            )
            old = dir_ref[rows, :]
            residual = res_ref[rows, :] - (image + load * old)
            new = keep * old + gain * residual
            total = sol_ref[rows, :] + new
            sol_ref[rows, :] = total
            if turn + 2 < ITERS:
                res_ref[rows, :] = residual
                dir_ref[rows, :] = new
                packed_ref[(turn + 1) % 2, rows, :] = new.astype(jnp.bfloat16)
            else:
                power = power + jnp.sum(total * total, axis=0, keepdims=True)

    power = (power[:, on_real] + power[:, on_imag]) / dish_total
    factor = lax.rsqrt((power + 1e-06) * dish_total)
    for rows in tiles:
        weight_real = (sol_ref[rows, on_real] * factor).astype(jnp.bfloat16).T
        weight_imag = (sol_ref[rows, on_imag] * factor).astype(jnp.bfloat16).T
        weight_ref[0, on_real, rows] = weight_real
        weight_ref[0, on_imag, rows] = -weight_imag
        weight_ref[1, on_real, rows] = weight_imag
        weight_ref[1, on_imag, rows] = weight_real

    for side in range(2):
        for first in range(0, span, TILE):
            place = side * span + first
            beams = jnp.dot(
                weight_ref[0],
                joined_ref[:, place : place + TILE],
                preferred_element_type=jnp.float32,
            ) + jnp.dot(
                weight_ref[1],
                joined_ref[:, frames + place : frames + place + TILE],
                preferred_element_type=jnp.float32,
            )
            beams = beams.astype(jnp.bfloat16)
            for part, lanes in enumerate((on_real, on_imag)):
                flipped = beams[lanes, :].T
                for group in range(TILE // half):
                    out_ref[first // half + group, part, side * half : (side + 1) * half, :] = (
                        flipped[group * half : (group + 1) * half, :]
                    )


def solve_call(sample_count, own, chan_index, loading, received, delay_rows):
    blocks, groups, _, half, _ = received.shape
    dish_total, beam_count = delay_rows.shape
    frames = 2 * groups * half
    smem = pl.BlockSpec(memory_space=pltpu.SMEM)
    vmem = pl.BlockSpec(memory_space=pltpu.VMEM)
    hbm = pl.BlockSpec(memory_space=pl.ANY)
    wide = (dish_total, 2 * beam_count)
    return pl.pallas_call(
        functools.partial(solve_kernel, sample_count),
        out_shape=jax.ShapeDtypeStruct((groups, 2, 2 * half, beam_count), jnp.bfloat16),
        in_specs=[smem, smem, smem, hbm, vmem],
        out_specs=vmem,
        scratch_shapes=[
            pltpu.VMEM(received.shape, jnp.bfloat16),
            pltpu.VMEM((dish_total, 2 * frames), jnp.bfloat16),
            pltpu.VMEM((dish_total, frames), jnp.bfloat16),
            pltpu.VMEM((dish_total, frames), jnp.bfloat16),
            pltpu.VMEM((dish_total, dish_total), jnp.float32),
            pltpu.VMEM((dish_total, dish_total), jnp.bfloat16),
            pltpu.VMEM((dish_total, dish_total), jnp.bfloat16),
            pltpu.VMEM((2,) + wide, jnp.bfloat16),
            pltpu.VMEM(wide, jnp.float32),
            pltpu.VMEM(wide, jnp.float32),
            pltpu.VMEM(wide, jnp.float32),
            pltpu.VMEM((2, 2 * beam_count, dish_total), jnp.bfloat16),
            pltpu.SemaphoreType.DMA((4,)),
        ],
        name="solve",
    )(own, chan_index, loading, received, delay_rows)


def local(samples, delays, loading, chan_index, dish_map, steer_index):
    dish_count = lax.axis_size("dish")
    chan_count = lax.axis_size("chan")
    own = (lax.axis_index("dish") * chan_count + lax.axis_index("chan")).reshape(1)
    spectra = spectra_call(samples, chan_index)
    received = lax.all_to_all(spectra, ("dish", "chan"), 0, 0, tiled=True)
    received = received.reshape((dish_count, chan_count) + received.shape[1:])
    delay_rows = jnp.take(jnp.take(delays, steer_index, axis=0), dish_map, axis=1).T
    beams = solve_call(samples.shape[2], own, chan_index, loading, received, delay_rows)
    return lax.all_to_all(beams, "chan", 0, 0, tiled=True).astype(jnp.float32)


def solution(mesh):
    return jax.shard_map(
        local,
        mesh=mesh,
        in_specs=(P("chan", "dish", None), P(), P(), P(), P(), P()),
        out_specs=P("dish", None, "chan", None),
        check_vma=False,
    )
```

```python
import math

import jax
import jax.numpy as jnp
from jax import lax
from jax.experimental import pallas as pl
from jax.experimental.pallas import tpu as pltpu
from jax.sharding import PartitionSpec as P

ITERS = 4
PIECES = (16, 16, 16, 16)
WIDE = 2
LANES = 128
TILE = 256
NT = (((1,), (1,)), ((), ()))


def sincos_turns(turns):
    quarter = jnp.round(turns * 4.0)
    angle = (turns - quarter * 0.25) * (2.0 * math.pi)
    square = angle * angle
    sine = angle * (
        1.0
        + square
        * (-1.0 / 6 + square * (1.0 / 120 + square * (-1.0 / 5040 + square * (1.0 / 362880))))
    )
    cosine = 1.0 + square * (
        -0.5
        + square
        * (
            1.0 / 24
            + square * (-1.0 / 720 + square * (1.0 / 40320 + square * (-1.0 / 3628800)))
        )
    )
    phase = quarter.astype(jnp.int32) & 3
    odd = (phase & 1) == 1
    cos_mag = jnp.where(odd, sine, cosine)
    sin_mag = jnp.where(odd, cosine, sine)
    cos_neg = (phase == 1) | (phase == 2)
    sin_neg = phase >= 2
    return jnp.where(cos_neg, -cos_mag, cos_mag), jnp.where(sin_neg, -sin_mag, sin_mag)


def spectra_kernel(
    chan_ref, samples_ref, out_ref, table_ref, held_ref, stage_ref, ready_ref, in_sems, out_sems
):
    selected = chan_ref.shape[1]
    sample_count = samples_ref.shape[3]
    half = samples_ref.shape[1]
    groups = out_sems.shape[0]
    pairs = half // groups

    loads = {}
    first = 0
    for piece, size in enumerate(PIECES):
        rows = slice(first, first + size)
        loads[first] = pltpu.make_async_copy(
            samples_ref.at[:, rows], held_ref.at[:, rows], in_sems.at[piece]
        )
        loads[first].start()
        first += size

    chan = jnp.broadcast_to(chan_ref[...].astype(jnp.float32), (selected, selected)).T
    position = lax.broadcasted_iota(jnp.int32, (selected, LANES), 1).astype(jnp.float32)
    turns = chan * position * (1.0 / sample_count)
    cosine, sine = sincos_turns(turns - jnp.round(turns))
    scaling = 1.0 / math.sqrt(sample_count)
    cosine = cosine * scaling
    sine = sine * scaling
    jump = chan * (float(LANES) / sample_count)
    jump_cos, jump_sin = sincos_turns(jump - jnp.round(jump))
    for block in range(sample_count // LANES):
        span = slice(block * LANES, (block + 1) * LANES)
        table_ref[0:selected, span] = cosine.astype(jnp.bfloat16)
        table_ref[selected : 2 * selected, span] = (-sine).astype(jnp.bfloat16)
        cosine, sine = (
            cosine * jump_cos - sine * jump_sin,
            sine * jump_cos + cosine * jump_sin,
        )

    stores = []
    stride = stage_ref.shape[1] // selected
    for group in range(groups):
        slot = group % 2
        for pair in range(0, pairs, WIDE):
            place = group * pairs + pair
            if place in loads:
                loads[place].wait()
            rows = jnp.concatenate(
                [held_ref[side, place + extra] for extra in range(WIDE) for side in range(2)],
                axis=0,
            )
            values = lax.dot_general(
                table_ref[...], rows, NT, preferred_element_type=jnp.float32
            )
            for extra in range(WIDE):
                for part in range(2):
                    stage_ref[
                        slot, pl.ds(part * pairs + pair + extra, selected, stride=stride), :
                    ] = values[
                        part * selected : (part + 1) * selected,
                        extra * LANES : (extra + 1) * LANES,
                    ]
        rows = slice(group * pairs, (group + 1) * pairs)
        staged = stage_ref[slot].reshape(selected, stride, LANES)[:, : 2 * pairs]
        ready_ref[:, :, rows] = staged.astype(jnp.bfloat16).reshape(selected, 2, pairs, LANES)
        stores.append(
            pltpu.make_async_copy(
                ready_ref.at[:, :, rows], out_ref.at[:, :, rows], out_sems.at[group]
            )
        )
        stores[-1].start()
    for store in stores:
        store.wait()


def spectra_call(samples, chan_index):
    frames, dishes, sample_count = samples.shape
    selected = chan_index.shape[0]
    half = frames // 2
    groups = 4
    stride = 2 * half // groups + 8
    hbm = pl.BlockSpec(memory_space=pl.ANY)
    return pl.pallas_call(
        spectra_kernel,
        out_shape=jax.ShapeDtypeStruct((selected, 2, half, LANES), jnp.bfloat16),
        in_specs=[pl.BlockSpec(memory_space=pltpu.VMEM), hbm],
        out_specs=hbm,
        scratch_shapes=[
            pltpu.VMEM((2 * selected, sample_count), jnp.bfloat16),
            pltpu.VMEM((2, half, dishes, sample_count), jnp.bfloat16),
            pltpu.VMEM((2, selected * stride, LANES), jnp.float32),
            pltpu.VMEM((selected, 2, half, LANES), jnp.bfloat16),
            pltpu.SemaphoreType.DMA((len(PIECES),)),
            pltpu.SemaphoreType.DMA((groups,)),
        ],
        name="spectra",
    )(chan_index.reshape(1, selected), samples.reshape(2, half, dishes, sample_count))


def solve_kernel(
    own_ref,
    load_ref,
    recv_ref,
    steer_ref,
    out_ref,
    held_ref,
    joined_ref,
    sum_ref,
    diff_ref,
    cross_ref,
    real_ref,
    imag_ref,
    packed_ref,
    sol_ref,
    res_ref,
    dir_ref,
    weight_ref,
    sems,
    steer_sem,
):
    blocks, groups, _, half, _ = recv_ref.shape
    dish_total, beam_count = steer_ref.shape[0], steer_ref.shape[1] // 2
    dish_local = dish_total // blocks
    span = groups * half
    frames = 2 * span
    own = own_ref[0]
    delta = load_ref[own]
    on_real, on_imag = slice(0, beam_count), slice(beam_count, 2 * beam_count)

    loads = []
    each = blocks // sems.shape[0]
    for index in range(sems.shape[0]):
        part = slice(index * each, (index + 1) * each)
        loads.append(pltpu.make_async_copy(recv_ref.at[part], held_ref.at[part], sems.at[index]))
        loads[-1].start()

    for block in range(blocks):
        if block % each == 0:
            loads[block // each].wait()
        rows = slice(block * dish_local, (block + 1) * dish_local)
        real_part, imag_part = (
            held_ref[block, :, part].reshape(span, LANES).T for part in range(2)
        )
        for side in range(2):
            inner = slice(side * dish_local, (side + 1) * dish_local)
            cols = slice(side * span, (side + 1) * span)
            joined_ref[rows, side * span : (side + 1) * span] = real_part[inner, :]
            joined_ref[rows, frames + side * span : frames + (side + 1) * span] = imag_part[
                inner, :
            ]
            sum_ref[rows, cols] = real_part[inner, :] + imag_part[inner, :]
            diff_ref[rows, cols] = real_part[inner, :] - imag_part[inner, :]

    steer_load = pltpu.make_async_copy(steer_ref, res_ref, steer_sem)
    steer_load.start()

    tiles = [slice(first, first + TILE) for first in range(0, dish_total, TILE)]
    same = lax.broadcasted_iota(jnp.int32, (TILE, TILE), 0) == lax.broadcasted_iota(
        jnp.int32, (TILE, TILE), 1
    )
    trace = jnp.zeros((1, TILE), jnp.float32)
    energy = jnp.zeros((1, TILE), jnp.float32)
    for index, cols in enumerate(tiles):
        top = cols.stop
        cross_ref[:, cols] = lax.dot_general(
            sum_ref[...], diff_ref[cols, :], NT, preferred_element_type=jnp.float32
        )
        square_imag = lax.dot_general(
            joined_ref[0:top, frames:],
            joined_ref[cols, frames:],
            NT,
            preferred_element_type=jnp.float32,
        )
        for rows in tiles[: index + 1]:
            upper_part = cross_ref[rows, cols]
            lower_part = cross_ref[cols, rows].T
            cov_real = 0.5 * (upper_part + lower_part) + 2.0 * square_imag[rows, :]
            cov_imag = 0.5 * (upper_part - lower_part)
            square = cov_real * cov_real + cov_imag * cov_imag
            share = jnp.sum(square, axis=0, keepdims=True)
            packed_real = cov_real.astype(jnp.bfloat16)
            packed_imag = cov_imag.astype(jnp.bfloat16)
            real_ref[rows, cols] = packed_real
            imag_ref[rows, cols] = packed_imag
            if rows == cols:
                diagonal = jnp.where(same, cov_real, 0.0)
                trace = trace + jnp.sum(diagonal, axis=0, keepdims=True)
                energy = energy + share
            else:
                energy = energy + 2.0 * share
                real_ref[cols, rows] = packed_real.T
                imag_ref[cols, rows] = -packed_imag.T

    steer_load.wait()

    def full(value):
        return jnp.full((1, 2 * beam_count), value, jnp.float32)

    scale_mean = full(jnp.sum(trace)) / dish_total + 1e-06
    load = full(delta)
    upper = load + jnp.sqrt(dish_total + full(jnp.sum(energy)) / (scale_mean * scale_mean))
    center = 0.5 * (upper + load)
    half_width = 0.5 * (upper - load)
    sigma = center / half_width
    inverse_scale = (1.0 / scale_mean)[:, on_real]
    inverse_center = 1.0 / center

    ratio_now = 1.0 / sigma
    power = jnp.zeros((1, 2 * beam_count), jnp.float32)
    for rows in tiles:
        first = res_ref[rows, :] * inverse_center
        sol_ref[rows, :] = first
        dir_ref[rows, :] = first
        packed_ref[0, rows, :] = first.astype(jnp.bfloat16)
    for turn in range(ITERS - 1):
        ratio_next = 1.0 / (2.0 * sigma - ratio_now)
        keep = ratio_next * ratio_now
        gain = 2.0 * ratio_next / half_width
        ratio_now = ratio_next
        packed = packed_ref[turn % 2]
        for rows in tiles:
            by_real = jnp.dot(real_ref[rows, :], packed, preferred_element_type=jnp.float32)
            by_imag = jnp.dot(imag_ref[rows, :], packed, preferred_element_type=jnp.float32)
            image = jnp.concatenate(
                [
                    (by_real[:, on_real] - by_imag[:, on_imag]) * inverse_scale,
                    (by_imag[:, on_real] + by_real[:, on_imag]) * inverse_scale,
                ],
                axis=1,
            )
            old = dir_ref[rows, :]
            residual = res_ref[rows, :] - (image + load * old)
            new = keep * old + gain * residual
            total = sol_ref[rows, :] + new
            sol_ref[rows, :] = total
            if turn + 2 < ITERS:
                res_ref[rows, :] = residual
                dir_ref[rows, :] = new
                packed_ref[(turn + 1) % 2, rows, :] = new.astype(jnp.bfloat16)
            else:
                power = power + jnp.sum(total * total, axis=0, keepdims=True)

    power = (power[:, on_real] + power[:, on_imag]) / dish_total
    factor = lax.rsqrt((power + 1e-06) * dish_total)
    for rows in tiles:
        weight_real = (sol_ref[rows, on_real] * factor).astype(jnp.bfloat16).T
        weight_imag = (sol_ref[rows, on_imag] * factor).astype(jnp.bfloat16).T
        weight_ref[0, on_real, rows] = weight_real
        weight_ref[0, on_imag, rows] = -weight_imag
        weight_ref[1, on_real, rows] = weight_imag
        weight_ref[1, on_imag, rows] = weight_real

    for side in range(2):
        for first in range(0, span, TILE):
            place = side * span + first
            beams = jnp.dot(
                weight_ref[0],
                joined_ref[:, place : place + TILE],
                preferred_element_type=jnp.float32,
            ) + jnp.dot(
                weight_ref[1],
                joined_ref[:, frames + place : frames + place + TILE],
                preferred_element_type=jnp.float32,
            )
            beams = beams.astype(jnp.bfloat16)
            for part, lanes in enumerate((on_real, on_imag)):
                flipped = beams[lanes, :].T
                for group in range(TILE // half):
                    out_ref[first // half + group, part, side * half : (side + 1) * half, :] = (
                        flipped[group * half : (group + 1) * half, :]
                    )


def solve_call(own, loading, received, steering):
    blocks, groups, _, half, _ = received.shape
    dish_total, beam_count = steering.shape[0], steering.shape[1] // 2
    frames = 2 * groups * half
    smem = pl.BlockSpec(memory_space=pltpu.SMEM)
    vmem = pl.BlockSpec(memory_space=pltpu.VMEM)
    hbm = pl.BlockSpec(memory_space=pl.ANY)
    wide = (dish_total, 2 * beam_count)
    return pl.pallas_call(
        solve_kernel,
        out_shape=jax.ShapeDtypeStruct((groups, 2, 2 * half, beam_count), jnp.bfloat16),
        in_specs=[smem, smem, hbm, hbm],
        out_specs=vmem,
        scratch_shapes=[
            pltpu.VMEM(received.shape, jnp.bfloat16),
            pltpu.VMEM((dish_total, 2 * frames), jnp.bfloat16),
            pltpu.VMEM((dish_total, frames), jnp.bfloat16),
            pltpu.VMEM((dish_total, frames), jnp.bfloat16),
            pltpu.VMEM((dish_total, dish_total), jnp.float32),
            pltpu.VMEM((dish_total, dish_total), jnp.bfloat16),
            pltpu.VMEM((dish_total, dish_total), jnp.bfloat16),
            pltpu.VMEM((2,) + wide, jnp.bfloat16),
            pltpu.VMEM(wide, jnp.float32),
            pltpu.VMEM(wide, jnp.float32),
            pltpu.VMEM(wide, jnp.float32),
            pltpu.VMEM((2, 2 * beam_count, dish_total), jnp.bfloat16),
            pltpu.SemaphoreType.DMA((4,)),
            pltpu.SemaphoreType.DMA(()),
        ],
        name="solve",
    )(own, loading, received, steering)


def local(samples, delays, loading, chan_index, dish_map, steer_index):
    dish_count = lax.axis_size("dish")
    chan_count = lax.axis_size("chan")
    own = (lax.axis_index("dish") * chan_count + lax.axis_index("chan")).reshape(1)
    spectra = spectra_call(samples, chan_index)
    received = lax.all_to_all(spectra, ("dish", "chan"), 0, 0, tiled=True)
    received = received.reshape((dish_count, chan_count) + received.shape[1:])
    delay_rows = jnp.take(jnp.take(delays, steer_index, axis=0), dish_map, axis=1).T
    bin_number = lax.dynamic_index_in_dim(chan_index, own[0], 0, False).astype(jnp.float32)
    turns = bin_number * delay_rows * (-1.0 / samples.shape[2])
    steering = jnp.concatenate(sincos_turns(turns - jnp.round(turns)), axis=1)
    beams = solve_call(own, loading, received, steering)
    return lax.all_to_all(beams, "chan", 0, 0, tiled=True).astype(jnp.float32)


def solution(mesh):
    return jax.shard_map(
        local,
        mesh=mesh,
        in_specs=(P("chan", "dish", None), P(), P(), P(), P(), P()),
        out_specs=P("dish", None, "chan", None),
        check_vma=False,
    )
```
